128 devices in a mesh: dp: 8 (over z_hi, x), rows: 16 (over y, z_lo, core).
Axes of the slice: x: 4, y: 4, z: 4 (z_hi: 2, z_lo: 2; z = z_hi * 2 + z_lo), core: 2. Of those that a mesh axis runs over, the one named last changes fastest.
Arguments:
- inputs: bfloat16 [8, 512, 64, 384], P('dp', 'rows'), may hold values from -6 to 6
- cotangent: bfloat16 [8, 512, 64, 384], P('dp', 'rows'), may hold values from -6 to 6
- weight_one: bfloat16 [3456, 384], replicated, may hold values from -0.109375 to 0.109375
- weight_two: bfloat16 [3456, 384], replicated, may hold values from -0.109375 to 0.109375
Outputs:
- output: bfloat16 [8, 512, 64, 384], P('dp', 'rows')
- grad_one: float32 [3456, 384], P('rows', 'dp')
- grad_two: float32 [3456, 384], P('rows', 'dp')
The draws below stay inside these ranges and needn't reach their ends.
All inputs are finite; a program needn't handle non-finite values.
Results may differ from the reference program's by a relative error of at most 0.006.
Values may be sent and summed in bfloat16 or wider, within the bound.
No kernel may reach another device: no remote copies, remote signals or barrier semaphores. Data moves between devices by JAX's collectives and lax.ppermute only.
A program may use at most 128 MiB of HBM per device.

```python
import math
import jax
import jax.numpy as jnp
from jax import lax

C = 384
H = 512
COLS = 64
DILATION_STEP = 32
SAMPLES = 8


def strengthened(entries, own_key, source, target, shards_of, factor):
    owner, partner = [(jnp.arange(entries.shape[dim]) // (entries.shape[dim] // shards_of)).reshape([-1 if axis == dim else 1 for axis in range(entries.ndim)]) for dim in (source, target)]
    chosen = jax.random.permutation(own_key, shards_of)[partner]
    strong = (owner == chosen) | (owner == (partner + shards_of // 2) % shards_of)
    return jnp.where(strong, factor * entries, entries)


def block_scale(own_key, shape, shards, low, top_value):
    factor_of, own = 1.0, jax.random.fold_in(own_key, 6)
    for position, parts in shards:
        steps = jnp.exp(jax.random.uniform(jax.random.fold_in(own, position), (parts,), jnp.float32, low / len(shards), top_value / len(shards)))
        factor_of = factor_of * jnp.repeat(steps, shape[position] // parts).reshape([-1 if axis == position else 1 for axis in range(len(shape))])
    return factor_of


def bell_draw(rng, shape, deviation, reach, cuts=(), kind=jnp.bfloat16):
    array = jax.random.normal(rng, shape, jnp.float32) * deviation
    if len(cuts) > 0:
        array = block_scale(rng, shape, cuts, -0.22, 0.18) * array
    return jnp.clip(array, min=-reach, max=reach).astype(kind)


def noise_with(rng, shape, deviation, most, shards, heavy, held_as=jnp.bfloat16):
    values = deviation * jax.random.normal(rng, shape, jnp.float32)
    if shards:
        values = values * block_scale(rng, shape, shards, -0.22, 0.18)
    return jnp.clip(strengthened(values, jax.random.fold_in(rng, 3), *heavy), -most, most).astype(held_as)


def setup_inputs(seed: int = 0) -> dict:
    streams_of = jax.random.split(jax.random.key(seed), 5)
    inputs = bell_draw(streams_of[0], (SAMPLES, H, COLS, C), 1.0, 6.0, ((0, 8), (1, 16)))
    cotangent = noise_with(streams_of[1], (SAMPLES, H, COLS, C), 1.0, 6.0, ((0, 8), (1, 16)), (0, 3, 8, 2.0))
    weight_one = bell_draw(streams_of[2], (9 * C, C), (9 * C) ** -0.5, 0.109375)
    weight_two = bell_draw(streams_of[3], (9 * C, C), (9 * C) ** -0.5, 0.109375)
    return dict(inputs=inputs, cotangent=cotangent, weight_one=weight_one, weight_two=weight_two)


def stack_taps(padded, count_rows, count_cols, pad_rows, pad_cols, step_rows, step_cols, direction):
    pieces = []
    for offset_row in (-1, 0, 1):
        for offset_col in (-1, 0, 1):
            first_row = pad_rows + direction * offset_row * step_rows
            first_col = pad_cols + direction * offset_col * step_cols
            pieces.append(padded[first_row:first_row + count_rows, first_col:first_col + count_cols, :])
    return jnp.concatenate(pieces, axis=-1)

def dilated_convolution(image, spacing, direction):
    padded = jnp.pad(image, ((spacing, spacing), (spacing, spacing), (0, 0)))
    return stack_taps(padded, image.shape[0], image.shape[1], spacing, spacing, spacing, spacing, direction)

def flipped(weights):
    channel_count = weights.shape[1]
    return jnp.transpose(weights.reshape(9, channel_count, channel_count), (0, 2, 1)).reshape(9 * channel_count, channel_count)

def contract(stacked, target):
    return lax.dot_general(stacked, target, (((0,), (0,)), ((), ())), preferred_element_type=jnp.float32)

def reference(inputs, cotangent, weight_one, weight_two):
    samples, height, width, channel_count = inputs.shape
    rotated_kernel = flipped(weight_two)

    def one_sample(pair):
        image, upstream_gradient = pair
        near = dilated_convolution(image, 4, 1).reshape(-1, 9 * channel_count)
        before = jnp.dot(near, weight_one, preferred_element_type=jnp.float32)
        hidden_state = jnp.maximum(before, 0.0).astype(jnp.bfloat16).reshape(height, width, channel_count)
        distant_frame = dilated_convolution(hidden_state, DILATION_STEP, 1).reshape(-1, 9 * channel_count)
        result = jnp.dot(distant_frame, weight_two, preferred_element_type=jnp.float32).astype(jnp.bfloat16)
        grad_two = contract(distant_frame, upstream_gradient.reshape(-1, channel_count))
        backward_signal = jnp.dot(dilated_convolution(upstream_gradient, DILATION_STEP, -1).reshape(-1, 9 * channel_count), rotated_kernel, preferred_element_type=jnp.float32).astype(jnp.bfloat16)
        masked = jnp.where(before > 0.0, backward_signal, jnp.zeros_like(backward_signal))
        grad_one = contract(near, masked)
        return (result.reshape(height, width, channel_count), grad_one, grad_two)
    outputs, grads_one, grads_two = lax.map(one_sample, (inputs, cotangent))
    factor = 1.0 / math.sqrt(samples * height * width)
    return (outputs, lax.optimization_barrier(jnp.sum(grads_one, axis=0)) * factor, lax.optimization_barrier(jnp.sum(grads_two, axis=0)) * factor)
```

```python
import functools
import math

import jax
import jax.numpy as jnp
from jax import lax
from jax.experimental import pallas as pl
from jax.experimental.pallas import tpu as pltpu
from jax.sharding import PartitionSpec as P


F32 = jnp.float32
BF16 = jnp.bfloat16
CH = 384
ROWS = 32
COLS = 64
HALF = 32
TAPS = 9 * CH
BLOCK = 216
SLIM = 48
WHOLE = pl.BlockSpec(memory_space=pltpu.VMEM)
AXES = ("dp", "rows")


def call(kernel, outs, args, flops=0, scratch=(), limit=8, aliases=None):
    single = not isinstance(outs, (list, tuple))
    shapes = [outs] if single else list(outs)
    moved = sum(a.size * a.dtype.itemsize for a in list(args) + shapes)
    run = pl.pallas_call(
        kernel,
        out_shape=shapes,
        in_specs=[WHOLE] * len(args),
        out_specs=[WHOLE] * len(shapes),
        scratch_shapes=list(scratch),
        input_output_aliases=aliases or {},
        compiler_params=pltpu.CompilerParams(vmem_limit_bytes=limit << 20),
        cost_estimate=pl.CostEstimate(flops=flops, bytes_accessed=moved, transcendentals=0),
    )
    result = run(*args)
    return result[0] if single else result


def shape_of(dims, kind):
    return jax.ShapeDtypeStruct(dims, kind)


def matmul(left, right):
    return jnp.dot(left, right, preferred_element_type=F32)


def place():
    dp = lax.axis_index("dp")
    rows = lax.axis_index("rows")
    return (
        lax.rem(dp, 4),
        lax.div(rows, 4),
        lax.rem(lax.div(rows, 2), 2),
        lax.div(dp, 4),
        lax.rem(rows, 2),
    )


def pairs_of(move):
    found = []
    for x in range(4):
        for y in range(4):
            for low in range(2):
                for high in range(2):
                    for core in range(2):
                        tx, ty, tl, th, tc = move(x, y, low, high, core)
                        source = (high * 4 + x) * 16 + (y * 2 + low) * 2 + core
                        target = (th * 4 + tx % 4) * 16 + ((ty % 4) * 2 + tl) * 2 + tc
                        found.append((source, target))
    return found


def send(block, move):
    return lax.ppermute(block, AXES, pairs_of(move))


def weight_kernel(w_ref, forward_ref, backward_ref):
    for a in range(3):
        zero = w_ref[pl.ds((3 * a + 1) * CH, CH)]
        minus = w_ref[pl.ds(3 * a * CH, CH)]
        plus = w_ref[pl.ds((3 * a + 2) * CH, CH)]
        parts = ((zero, minus), (plus, zero))
        for i in range(2):
            for j in range(2):
                forward_ref[pl.ds((2 * a + i) * CH, CH), pl.ds(j * CH, CH)] = parts[i][j]
                backward_ref[pl.ds((2 * a + j) * CH, CH), pl.ds(i * CH, CH)] = parts[i][j].T


def shifted_store(near_ref, first, value):
    count = value.shape[0]
    zeros = jnp.zeros((count, 4, CH), BF16)
    near_ref[0, pl.ds(first, count)] = jnp.concatenate([zeros, value[:, : COLS - 4]], axis=1)
    near_ref[1, pl.ds(first, count)] = value
    near_ref[2, pl.ds(first, count)] = jnp.concatenate([value[:, 4:], zeros], axis=1)


def near_rows(near_ref, w_ref, hidden_ref, first, count):
    total = None
    for a in range(3):
        for b in range(3):
            window = near_ref[b, pl.ds(first + 4 * a, count)].reshape(count * COLS, CH)
            product = matmul(window, w_ref[pl.ds((3 * a + b) * CH, CH)])
            total = product if total is None else total + product
    hidden_ref[pl.ds(first, count)] = (
        jnp.maximum(total, 0.0).astype(BF16).reshape(count, COLS, CH)
    )


def near_mid_kernel(own_ref, w_ref, hidden_ref, near_ref):
    @pl.loop(0, ROWS // 4)
    def _(i):
        shifted_store(near_ref, 4 + i * 4, own_ref[pl.ds(i * 4, 4)])

    @pl.loop(0, 3)
    def _(m):
        near_rows(near_ref, w_ref, hidden_ref, 4 + m * 8, 8)


def near_edge_kernel(distant_ref, chip_ref, w_ref, mid_ref, wide_ref, hidden_ref, near_ref):
    core = place()[4]
    shifted_store(near_ref, (ROWS + 4) * core, distant_ref[...])
    shifted_store(near_ref, (ROWS + 4) * (1 - core), chip_ref[...])

    @pl.loop(0, 2)
    def _(m):
        near_rows(near_ref, w_ref, hidden_ref, m * (ROWS - 4), 4)


def side_rows(ref, first, chunk):
    return jnp.concatenate(
        [
            ref[pl.ds(first, chunk), pl.ds(side * HALF, HALF)].reshape(chunk * HALF, CH)
            for side in range(2)
        ],
        axis=1,
    )


def block_of(w_ref, at):
    return w_ref[pl.ds(pl.multiple_of(at * 2 * CH, 16), 2 * CH)]


def far_start_kernel(flip, own_ref, chip_ref, w_ref, total_ref):
    core = place()[4]
    at = 2 * core if flip else 2 - 2 * core
    chunk = 16

    @pl.loop(0, ROWS // chunk)
    def _(m):
        total = matmul(side_rows(own_ref, m * chunk, chunk), block_of(w_ref, 1))
        total = total + matmul(side_rows(chip_ref, m * chunk, chunk), block_of(w_ref, at))
        for side in range(2):
            total_ref[pl.ds(m * chunk, chunk), pl.ds(side * HALF, HALF)] = total[
                :, side * CH : (side + 1) * CH
            ].reshape(chunk, HALF, CH)


PART = ROWS // 2


def distant_part(distant_ref, w_ref, at, first, chunk):
    return matmul(side_rows(distant_ref, first, chunk), block_of(w_ref, at))


def conv_end_kernel(total_ref, distant_ref, w_ref, out_ref):
    core = place()[4]
    chunk = 16

    @pl.loop(0, ROWS // chunk)
    def _(m):
        total = distant_part(distant_ref, w_ref, 2 * core, m * chunk, chunk)
        for side in range(2):
            where = (pl.ds(m * chunk, chunk), pl.ds(side * HALF, HALF))
            part = total[:, side * CH : (side + 1) * CH].reshape(chunk, HALF, CH)
            out_ref[where] = (total_ref[where] + part).astype(BF16)


def back_end_kernel(index, total_ref, distant_ref, w_ref, hidden_ref, out_ref):
    core = place()[4]
    total = distant_part(distant_ref, w_ref, 2 - 2 * core, 0, PART)
    for side in range(2):
        cols = slice(side * HALF, (side + 1) * HALF)
        where = (slice(index * PART, (index + 1) * PART), cols)
        part = total[:, side * CH : (side + 1) * CH].reshape(PART, HALF, CH)
        value = (total_ref[where] + part).astype(BF16)
        out_ref[:, cols] = jnp.where(hidden_ref[where] > 0, value, jnp.zeros_like(value))


def split_cores(full_ref, keep_ref, send_ref):
    core = place()[4]
    for j in range(8):
        mine = full_ref[pl.ds(pl.multiple_of((2 * j + core) * BLOCK, 8), BLOCK)]
        other = full_ref[pl.ds(pl.multiple_of((2 * j + 1 - core) * BLOCK, 8), BLOCK)]
        keep_ref[j // 2, j % 2] = mine
        send_ref[j // 2, j % 2] = other.astype(BF16)


def outer(left, right):
    return lax.dot_general(left, right, (((0,), (0,)), ((), ())), preferred_element_type=F32)


def fill_halves(ref, out_ref):
    for side in range(2):
        out_ref[:, side * CH : (side + 1) * CH] = ref[
            :, side * HALF : (side + 1) * HALF
        ].reshape(ROWS * HALF, CH)


def taps_at(full_ref, at):
    return full_ref.at[pl.ds(pl.multiple_of(at * 3 * CH, 16), 3 * CH)]


def outer_taps(h_ref, c_ref, target):
    grad = outer(h_ref[...], c_ref[...])
    target[0:CH] = grad[:CH, CH:]
    target[CH : 2 * CH] = grad[:CH, :CH] + grad[CH:, CH:]
    target[2 * CH :] = grad[CH:, :CH]


def grad_start_kernel(hidden_ref, own_ref, chip_ref, full_ref, h_ref, c_ref):
    core = place()[4]
    fill_halves(hidden_ref, h_ref)
    fill_halves(own_ref, c_ref)
    outer_taps(h_ref, c_ref, taps_at(full_ref, 1))
    fill_halves(chip_ref, c_ref)
    outer_taps(h_ref, c_ref, taps_at(full_ref, 2 * core))


def fill_part(ref, first, out_ref):
    for side in range(2):
        out_ref[:, side * CH : (side + 1) * CH] = ref[
            first : first + PART, side * HALF : (side + 1) * HALF
        ].reshape(PART * HALF, CH)


def grad_part_kernel(hidden_ref, distant_ref, part_ref, h_ref, c_ref):
    fill_part(hidden_ref, 0, h_ref)
    fill_part(distant_ref, 0, c_ref)
    outer_taps(h_ref, c_ref, part_ref)


def grad_end_kernel(
    begun_ref, part_ref, hidden_ref, distant_ref, keep_ref, send_ref, h_ref, c_ref, full_ref
):
    core = place()[4]
    fill_part(hidden_ref, PART, h_ref)
    fill_part(distant_ref, 0, c_ref)
    target = taps_at(full_ref, 2 - 2 * core)
    outer_taps(h_ref, c_ref, target)
    target[...] = target[...] + part_ref[...]
    for at in (1, 2 * core):
        taps_at(full_ref, at)[...] = taps_at(begun_ref, at)[...]
    split_cores(full_ref, keep_ref, send_ref)


def near_window(near_ref, index, a, b):
    first = 4 * a + index * PART
    return near_ref[b, first : first + PART].reshape(PART * COLS, CH)


def near_part_kernel(near_ref, masked_ref, part_ref):
    target = masked_ref[...].reshape(PART * COLS, CH)
    for a in range(3):
        for b in range(3):
            part_ref[pl.ds((3 * a + b) * CH, CH)] = outer(near_window(near_ref, 0, a, b), target)


def near_end_kernel(part_ref, near_ref, masked_ref, keep_ref, send_ref, full_ref):
    target = masked_ref[...].reshape(PART * COLS, CH)
    for a in range(3):
        for b in range(3):
            where = pl.ds((3 * a + b) * CH, CH)
            full_ref[where] = part_ref[where] + outer(near_window(near_ref, 1, a, b), target)
    split_cores(full_ref, keep_ref, send_ref)


BANDS = tuple((at, min(48, BLOCK - at)) for at in range(0, BLOCK, 48))


def one_first_kernel(keep_ref, got_ref, own_ref, p1, p2, p3, hold_ref):
    x = place()[0]
    for at, count in BANDS:
        band = slice(at, at + count)
        lane = lax.broadcasted_iota(jnp.int32, (count, CH), 1)
        lane = jnp.where(lane >= 4 * SLIM, lane - 4 * SLIM, lane)
        for low in range(2):
            turned = []
            for y in range(4):
                total = keep_ref[y, low, band] + got_ref[y, low, band].astype(F32)
                turned.append(pltpu.roll(total, SLIM * y, 1) if y else total)
            for q in range(4):
                part = turned[(3 - q) % 4]
                for r in (2, 1, 0):
                    part = jnp.where(lane < (r + 1) * SLIM, turned[(r - q) % 4], part)
                hold_ref[q, low, band] = part
    own_ref[...] = hold_ref[x]
    for k, ref in enumerate((p1, p2, p3)):
        ref[...] = hold_ref[lax.rem(x + k + 1, 4)].astype(BF16)


def two_first_kernel(keep_ref, got_ref, *refs):
    y = place()[1]
    for k, ref in enumerate(refs):
        at = lax.rem(y + k, 4)
        ref[...] = (keep_ref[at] + got_ref[at].astype(F32)).astype(ref.dtype)


def second_kernel(turned, kept_ref, r1, r2, r3, own_ref, p1, p2, p3, hold_ref):
    x, y = place()[:2]
    base = x + y if turned else x
    for at, count in BANDS:
        band = slice(at, at + count)
        for low in range(2):
            total = kept_ref[low, band]
            for r in (r1, r2, r3):
                total = total + r[low, band].astype(F32)
            for q in range(4):
                for side in range(2):
                    start = side * 4 * SLIM + q * SLIM
                    to = (2 * low + side) * SLIM
                    hold_ref[q, band, to : to + SLIM] = total[:, start : start + SLIM]
    own_ref[...] = hold_ref[lax.rem(base, 4)]
    for k, ref in enumerate((p1, p2, p3)):
        ref[...] = hold_ref[lax.rem(base + k + 1, 4)].astype(BF16)


def third_kernel(*refs):
    ins, (own_ref, p1, p2, p3, hold_ref) = refs[:8], refs[8:]
    x, y, low, high, _ = place()
    for g in range(2):
        kept, *got = ins[4 * g : 4 * g + 4]
        total = kept[...]
        for ref in got:
            total = total + ref[...].astype(F32)
        for l in range(2):
            for side in range(2):
                at = (2 * l + side) * SLIM
                hold_ref[g, l, side] = total[:, at : at + SLIM]
        here = high if g else lax.rem(high + lax.div(x + y, 4), 2)
        spots = ((low, here), (1 - low, here), (low, 1 - here), (1 - low, 1 - here))
        for ref, (l, side) in zip((own_ref, p1, p2, p3), spots):
            ref[:, g * SLIM : (g + 1) * SLIM] = hold_ref[g, l, side].astype(ref.dtype)


def last_kernel(factor, kept_ref, r1, r2, r3, one_ref, two_ref):
    total = kept_ref[...]
    for ref in (r1, r2, r3):
        total = total + ref[...].astype(F32)
    total = total * factor
    one_ref[...] = total[:, 0:SLIM]
    two_ref[...] = total[:, SLIM : 2 * SLIM]


def pieces_of(dims):
    return [shape_of(dims, F32)] + [shape_of(dims, BF16)] * 3


def swap_core(block):
    return send(block, lambda x, y, l, h, c: (x, y, l, h, 1 - c))


def over_x(pieces):
    own, *pieces = pieces
    result = [own]
    for k, piece in enumerate(pieces):
        result.append(send(piece, lambda x, y, l, h, c: (x + k + 1, y, l, h, c)))
    return result


def over_y(pieces):
    own, *pieces = pieces
    result = [own]
    for k, piece in enumerate(pieces):
        result.append(send(piece, lambda x, y, l, h, c: (x, y + k + 1, l, h, c)))
    return result


def second_stage(turned, held):
    dims = (BLOCK, 4 * SLIM)
    return call(
        functools.partial(second_kernel, turned),
        pieces_of(dims),
        held,
        scratch=[pltpu.VMEM((4, *dims), F32)],
    )


def reduce_grads(keep_one, send_one, keep_two, send_two, factor):
    got_one = swap_core(send_one)
    got_two = swap_core(send_two)
    dims = (2, BLOCK, CH)
    one = call(
        one_first_kernel,
        pieces_of(dims),
        (keep_one, got_one),
        scratch=[pltpu.VMEM((4, *dims), F32)],
    )
    two = call(two_first_kernel, pieces_of(dims), (keep_two, got_two))
    one = second_stage(True, over_x(one))
    two = second_stage(False, over_y(two))
    one = over_y(one)
    two = over_x(two)
    dims = (BLOCK, 2 * SLIM)
    own, *pieces = call(
        third_kernel,
        pieces_of(dims),
        (*one, *two),
        scratch=[pltpu.VMEM((2, 2, 2, BLOCK, SLIM), F32)],
    )
    moves = (
        lambda x, y, l, h, c: (x, y, 1 - l, h, c),
        lambda x, y, l, h, c: (x, y, l, 1 - h, c),
        lambda x, y, l, h, c: (x, y, 1 - l, 1 - h, c),
    )
    got = []
    for piece, move in zip(pieces, moves):
        got.append(send(piece, move))
    kind = shape_of((BLOCK, SLIM), F32)
    return call(functools.partial(last_kernel, factor), [kind, kind], (own, *got))


def swap_chip(block):
    return send(block, lambda x, y, l, h, c: (x, y, l, h, 1 - c))


def swap_distant(block):
    count = lax.axis_size("rows")
    pairs = [(i, i + 1) for i in range(1, count - 1, 2)]
    return lax.ppermute(block, "rows", pairs + [(j, i) for i, j in pairs])


def swap_in_steps(block):
    count = lax.axis_size("rows")
    pairs = [(i, i) for i in range(count) if i % 4 in (1, 2)]
    for i in range(3, count - 1, 4):
        pairs += [(i, i + 4), (i + 1, i - 3)]
    block = lax.ppermute(block, "rows", pairs)
    return lax.ppermute(block, "rows", [(i, i ^ 3) for i in range(count)])


def on_device(inputs, cotangent, weight_one, weight_two):
    picture = inputs[0]
    upstream = cotangent[0]
    factor = 1.0 / math.sqrt(lax.axis_size("dp") * ROWS * lax.axis_size("rows") * COLS)
    work = 2 * ROWS * COLS * CH * CH
    first_core = lax.rem(lax.axis_index("rows"), 2) == 0
    head, tail = picture[:4], picture[-4:]
    edge_distant = swap_distant(jnp.where(first_core, head, tail))
    c_parts = [swap_distant(upstream[i * PART : (i + 1) * PART]) for i in range(2)]
    edge_chip = swap_chip(jnp.where(first_core, tail, head))
    c_chip = swap_chip(upstream)
    kind = shape_of((6 * CH, 2 * CH), BF16)
    forward_w, backward_w = call(weight_kernel, [kind, kind], (weight_two,))
    map_kind = shape_of((ROWS, COLS, CH), BF16)
    part_kind = shape_of((PART, COLS, CH), BF16)
    sum_kind = shape_of((ROWS, COLS, CH), F32)
    wide_kind = shape_of((3, ROWS + 8, COLS, CH), BF16)
    hidden, near = call(
        near_mid_kernel, [map_kind, wide_kind], (picture, weight_one), flops=7 * work
    )
    hidden, near = call(
        near_edge_kernel,
        [map_kind, wide_kind],
        (edge_distant, edge_chip, weight_one, hidden, near),
        flops=2 * work,
        aliases={3: 0, 4: 1},
    )
    h_chip = swap_chip(hidden)
    h_distant = swap_in_steps(hidden)
    full = pltpu.VMEM((TAPS, CH), F32)
    halves = [pltpu.VMEM((ROWS * HALF, 2 * CH), BF16)] * 2
    parts = [pltpu.VMEM((PART * HALF, 2 * CH), BF16)] * 2
    block_kinds = [shape_of((4, 2, BLOCK, CH), F32), shape_of((4, 2, BLOCK, CH), BF16)]
    begun = call(
        grad_start_kernel,
        shape_of((TAPS, CH), F32),
        (hidden, upstream, c_chip),
        flops=4 * work,
        scratch=halves,
    )
    back = call(
        functools.partial(far_start_kernel, True),
        sum_kind,
        (upstream, c_chip, backward_w),
        flops=4 * work,
    )
    result = call(
        functools.partial(far_start_kernel, False),
        sum_kind,
        (hidden, h_chip, forward_w),
        flops=4 * work,
    )
    masked = [
        call(
            functools.partial(back_end_kernel, i),
            part_kind,
            (back, c_parts[i], backward_w, hidden),
            flops=work,
        )
        for i in range(2)
    ]
    near_part = call(near_part_kernel, shape_of((TAPS, CH), F32), (near, masked[0]), flops=4 * work)
    grad_part = call(
        grad_part_kernel,
        shape_of((3 * CH, CH), F32),
        (hidden, c_parts[0]),
        flops=work,
        scratch=parts,
    )
    keep_one, send_one = call(
        near_end_kernel,
        block_kinds,
        (near_part, near, masked[1]),
        flops=5 * work,
        scratch=[full],
        limit=12,
    )
    keep_two, send_two = call(
        grad_end_kernel,
        block_kinds,
        (begun, grad_part, hidden, c_parts[1]),
        flops=work,
        scratch=[*parts, full],
        limit=12,
    )
    grad_one, grad_two = reduce_grads(keep_one, send_one, keep_two, send_two, factor)
    output = call(conv_end_kernel, map_kind, (result, h_distant, forward_w), flops=2 * work)
    return (output[None], grad_one, grad_two)


def solution(mesh):
    return jax.shard_map(
        on_device,
        mesh=mesh,
        in_specs=(P("dp", "rows", None, None), P("dp", "rows", None, None), P(), P()),
        out_specs=(P("dp", "rows", None, None), P("rows", "dp"), P("rows", "dp")),
        check_vma=False,
    )
```

```python
import functools
import math

import jax
import jax.numpy as jnp
from jax import lax
from jax.experimental import pallas as pl
from jax.experimental.pallas import tpu as pltpu
from jax.sharding import PartitionSpec as P


F32 = jnp.float32
BF16 = jnp.bfloat16
CH = 384
ROWS = 32
COLS = 64
HALF = 32
TAPS = 9 * CH
BLOCK = 216
SLIM = 48
TALL = 112
WHOLE = pl.BlockSpec(memory_space=pltpu.VMEM)
PARTS = ((0, 20), (20, 12))
AXES = ("dp", "rows")


def call(kernel, outs, args, flops=0, scratch=(), limit=8, aliases=None, where=None):
    single = not isinstance(outs, (list, tuple))
    shapes = [outs] if single else list(outs)
    moved = sum(a.size * a.dtype.itemsize for a in list(args) + shapes)
    run = pl.pallas_call(
        kernel,
        out_shape=shapes,
        in_specs=where or [WHOLE] * len(args),
        out_specs=[WHOLE] * len(shapes),
        scratch_shapes=list(scratch),
        input_output_aliases=aliases or {},
        compiler_params=pltpu.CompilerParams(vmem_limit_bytes=limit << 20),
        cost_estimate=pl.CostEstimate(flops=flops, bytes_accessed=moved, transcendentals=0),
    )
    result = run(*args)
    return result[0] if single else result


def shape_of(dims, kind):
    return jax.ShapeDtypeStruct(dims, kind)


def matmul(left, right):
    return jnp.dot(left, right, preferred_element_type=F32)


def place():
    dp = lax.axis_index("dp")
    rows = lax.axis_index("rows")
    return (
        lax.rem(dp, 4),
        lax.div(rows, 4),
        lax.rem(lax.div(rows, 2), 2),
        lax.div(dp, 4),
        lax.rem(rows, 2),
    )


def pairs_of(move):
    found = []
    for x in range(4):
        for y in range(4):
            for low in range(2):
                for high in range(2):
                    for core in range(2):
                        tx, ty, tl, th, tc = move(x, y, low, high, core)
                        source = (high * 4 + x) * 16 + (y * 2 + low) * 2 + core
                        target = (th * 4 + tx % 4) * 16 + ((ty % 4) * 2 + tl) * 2 + tc
                        found.append((source, target))
    return found


def send(block, move):
    return lax.ppermute(block, AXES, pairs_of(move))


def weight_kernel(w_ref, forward_ref, backward_ref):
    for a in range(3):
        zero = w_ref[pl.ds((3 * a + 1) * CH, CH)]
        minus = w_ref[pl.ds(3 * a * CH, CH)]
        plus = w_ref[pl.ds((3 * a + 2) * CH, CH)]
        parts = ((zero, minus), (plus, zero))
        for i in range(2):
            for j in range(2):
                forward_ref[pl.ds((2 * a + i) * CH, CH), pl.ds(j * CH, CH)] = parts[i][j]
                backward_ref[pl.ds((2 * a + j) * CH, CH), pl.ds(i * CH, CH)] = parts[i][j].T


def shifted_store(near_ref, first, value):
    count = value.shape[0]
    zeros = jnp.zeros((count, 4, CH), BF16)
    near_ref[0, pl.ds(first, count)] = jnp.concatenate([zeros, value[:, : COLS - 4]], axis=1)
    near_ref[1, pl.ds(first, count)] = value
    near_ref[2, pl.ds(first, count)] = jnp.concatenate([value[:, 4:], zeros], axis=1)


def near_rows(near_ref, w_ref, hidden_ref, first, count):
    total = None
    for a in range(3):
        for b in range(3):
            window = near_ref[b, pl.ds(first + 4 * a, count)].reshape(count * COLS, CH)
            product = matmul(window, w_ref[pl.ds((3 * a + b) * CH, CH)])
            total = product if total is None else total + product
    hidden_ref[pl.ds(first, count)] = (
        jnp.maximum(total, 0.0).astype(BF16).reshape(count, COLS, CH)
    )


def near_mid_kernel(own_ref, far_ref, hidden_ref, near_ref, w_ref, sem):
    copy = pltpu.make_async_copy(far_ref, w_ref, sem)
    copy.start()

    @pl.loop(0, ROWS // 4)
    def _(i):
        shifted_store(near_ref, 4 + i * 4, own_ref[pl.ds(i * 4, 4)])

    copy.wait()

    @pl.loop(0, 3)
    def _(m):
        near_rows(near_ref, w_ref, hidden_ref, 4 + m * 8, 8)


def near_edge_kernel(distant_ref, chip_ref, w_ref, mid_ref, wide_ref, hidden_ref, near_ref):
    core = place()[4]
    shifted_store(near_ref, (ROWS + 4) * core, distant_ref[...])
    shifted_store(near_ref, (ROWS + 4) * (1 - core), chip_ref[...])

    @pl.loop(0, 2)
    def _(m):
        near_rows(near_ref, w_ref, hidden_ref, m * (ROWS - 4), 4)


def side_rows(ref, first, chunk):
    return jnp.concatenate(
        [
            ref[pl.ds(first, chunk), pl.ds(side * HALF, HALF)].reshape(chunk * HALF, CH)
            for side in range(2)
        ],
        axis=1,
    )


def block_of(w_ref, at):
    return w_ref[pl.ds(pl.multiple_of(at * 2 * CH, 16), 2 * CH)]


def far_start_kernel(flip, own_ref, chip_ref, w_ref, total_ref):
    core = place()[4]
    at = 2 * core if flip else 2 - 2 * core
    chunk = 16

    @pl.loop(0, ROWS // chunk)
    def _(m):
        total = matmul(side_rows(own_ref, m * chunk, chunk), block_of(w_ref, 1))
        total = total + matmul(side_rows(chip_ref, m * chunk, chunk), block_of(w_ref, at))
        for side in range(2):
            total_ref[pl.ds(m * chunk, chunk), pl.ds(side * HALF, HALF)] = total[
                :, side * CH : (side + 1) * CH
            ].reshape(chunk, HALF, CH)


def distant_part(distant_ref, w_ref, at, first, chunk):
    return matmul(side_rows(distant_ref, first, chunk), block_of(w_ref, at))


def conv_end_kernel(total_ref, distant_ref, w_ref, out_ref):
    core = place()[4]
    chunk = 16

    @pl.loop(0, ROWS // chunk)
    def _(m):
        total = distant_part(distant_ref, w_ref, 2 * core, m * chunk, chunk)
        for side in range(2):
            where = (pl.ds(m * chunk, chunk), pl.ds(side * HALF, HALF))
            part = total[:, side * CH : (side + 1) * CH].reshape(chunk, HALF, CH)
            out_ref[where] = (total_ref[where] + part).astype(BF16)


def back_end_kernel(first, count, total_ref, distant_ref, w_ref, hidden_ref, out_ref):
    core = place()[4]
    total = distant_part(distant_ref, w_ref, 2 - 2 * core, 0, count)
    for side in range(2):
        cols = slice(side * HALF, (side + 1) * HALF)
        where = (slice(first, first + count), cols)
        part = total[:, side * CH : (side + 1) * CH].reshape(count, HALF, CH)
        value = (total_ref[where] + part).astype(BF16)
        out_ref[:, cols] = jnp.where(hidden_ref[where] > 0, value, jnp.zeros_like(value))


def block_at(full_ref, y, low, core, at=0, count=BLOCK):
    first = pl.multiple_of((4 * y + 2 * low + core) * BLOCK + at, 8)
    return full_ref[pl.ds(first, count)]


def fill_send(full_ref, send_ref):
    core = place()[4]
    for y in range(4):
        for low in range(2):
            send_ref[y, low] = block_at(full_ref, y, low, 1 - core).astype(BF16)


def outer(left, right):
    return lax.dot_general(left, right, (((0,), (0,)), ((), ())), preferred_element_type=F32)


def fill_halves(ref, out_ref):
    for side in range(2):
        out_ref[:, side * CH : (side + 1) * CH] = ref[
            :, side * HALF : (side + 1) * HALF
        ].reshape(ROWS * HALF, CH)


def taps_at(full_ref, at):
    return full_ref.at[pl.ds(pl.multiple_of(at * 3 * CH, 16), 3 * CH)]


def outer_taps(h_ref, c_ref, target):
    grad = outer(h_ref[...], c_ref[...])
    target[0:CH] = grad[:CH, CH:]
    target[CH : 2 * CH] = grad[:CH, :CH] + grad[CH:, CH:]
    target[2 * CH :] = grad[CH:, :CH]


def grad_start_kernel(hidden_ref, own_ref, chip_ref, full_ref, h_ref, c_ref):
    core = place()[4]
    fill_halves(hidden_ref, h_ref)
    fill_halves(own_ref, c_ref)
    outer_taps(h_ref, c_ref, taps_at(full_ref, 1))
    fill_halves(chip_ref, c_ref)
    outer_taps(h_ref, c_ref, taps_at(full_ref, 2 * core))


def fill_part(ref, first, out_ref):
    count = out_ref.shape[0] // HALF
    for side in range(2):
        out_ref[:, side * CH : (side + 1) * CH] = ref[
            first : first + count, side * HALF : (side + 1) * HALF
        ].reshape(count * HALF, CH)


def grad_part_kernel(first, hidden_ref, distant_ref, begun_ref, full_ref, *refs):
    core = place()[4]
    h_ref, c_ref = refs[-2:]
    fill_part(hidden_ref, first, h_ref)
    fill_part(distant_ref, 0, c_ref)
    grad = outer(h_ref[...], c_ref[...])
    target = taps_at(full_ref, 2 - 2 * core)
    terms = (grad[:CH, CH:], grad[:CH, :CH] + grad[CH:, CH:], grad[CH:, :CH])
    for b, term in enumerate(terms):
        where = slice(b * CH, (b + 1) * CH)
        target[where] = target[where] + term if first else term
    if len(refs) == 3:
        fill_send(full_ref, refs[0])


def near_part_kernel(first, count, near_ref, masked_ref, *refs):
    if first:
        refs = refs[1:]
    full_ref = refs[0]
    target = masked_ref[...].reshape(count * COLS, CH)
    for a in range(3):
        for b in range(3):
            start = 4 * a + first
            window = near_ref[b, start : start + count].reshape(count * COLS, CH)
            where = pl.ds((3 * a + b) * CH, CH)
            term = outer(window, target)
            full_ref[where] = full_ref[where] + term if first else term
    if len(refs) == 2:
        fill_send(full_ref, refs[1])


BANDS = tuple((at, min(48, BLOCK - at)) for at in range(0, BLOCK, 48))


def partners(spot, core):
    return spot ^ (1 + 2 * core), spot ^ (3 - 2 * core), spot ^ 2


def hand_out(piece, spot, core, own_ref, other_ref, send_ref):
    near, later, across = partners(spot, core)
    own_ref[...] = piece(spot)
    other_ref[...] = piece(later)
    send_ref[0] = piece(near).astype(BF16)
    send_ref[1] = piece(across).astype(BF16)


def one_first_kernel(full_ref, got_ref, own_ref, other_ref, send_ref, hold_ref):
    x, _, _, _, core = place()
    for at, count in BANDS:
        band = slice(at, at + count)
        lane = lax.broadcasted_iota(jnp.int32, (count, CH), 1)
        lane = jnp.where(lane >= 4 * SLIM, lane - 4 * SLIM, lane)
        for low in range(2):
            turned = []
            for y in range(4):
                total = block_at(full_ref, y, low, core, at, count)
                total = total + got_ref[y, low, band].astype(F32)
                turned.append(pltpu.roll(total, SLIM * y, 1) if y else total)
            for q in range(4):
                part = turned[(3 - q) % 4]
                for r in (2, 1, 0):
                    part = jnp.where(lane < (r + 1) * SLIM, turned[(r - q) % 4], part)
                hold_ref[q, low, band] = part
    hand_out(lambda q: hold_ref[q], x, core, own_ref, other_ref, send_ref)


def two_first_kernel(full_ref, got_ref, own_ref, other_ref, send_ref):
    _, y, _, _, core = place()
    near, later, across = partners(y, core)
    spots = ((own_ref, y), (other_ref, later), (send_ref.at[0], near), (send_ref.at[1], across))
    for ref, at in spots:
        for low in range(2):
            total = block_at(full_ref, at, low, core) + got_ref[at, low].astype(F32)
            ref[low] = total.astype(ref.dtype)


def middle_kernel(other_ref, got_ref, out_ref):
    out_ref[...] = (other_ref[...] + got_ref[1].astype(F32)).astype(BF16)


PACKS = ((0, 48), (48, 48), (96, 16), (112, 48), (160, 48), (208, 8))


def second_kernel(turned, kept_ref, got_ref, last_ref, own_ref, p1, p2, p3, hold_ref):
    x, y = place()[:2]
    base = x + y if turned else x
    for at, count in PACKS:
        band = slice(at, at + count)
        right = at >= TALL
        rows = slice(at - TALL, at - TALL + count) if right else band
        for low in range(2):
            total = kept_ref[low, band] + got_ref[0, low, band].astype(F32)
            total = total + last_ref[low, band].astype(F32)
            for q in range(4):
                for side in range(2):
                    start = side * 4 * SLIM + q * SLIM
                    to = (4 * right + 2 * low + side) * SLIM
                    hold_ref[q, rows, to : to + SLIM] = total[:, start : start + SLIM]
    own_ref[...] = hold_ref[lax.rem(base, 4)]
    for k, ref in enumerate((p1, p2, p3)):
        ref[...] = hold_ref[lax.rem(base + k + 1, 4)].astype(BF16)


def third_kernel(*refs):
    ins, (own_ref, p1, p2, p3, hold_ref) = refs[:8], refs[8:]
    x, y, low, high, _ = place()
    for g in range(2):
        kept, *got = ins[4 * g : 4 * g + 4]
        total = kept[...]
        for ref in got:
            total = total + ref[...].astype(F32)
        for l in range(2):
            for side in range(2):
                at = (2 * l + side) * SLIM
                hold_ref[g, l, side, 0:TALL] = total[:, at : at + SLIM]
                at = at + 4 * SLIM
                hold_ref[g, l, side, TALL:BLOCK] = total[: BLOCK - TALL, at : at + SLIM]
        here = high if g else lax.rem(high + lax.div(x + y, 4), 2)
        spots = ((low, here), (1 - low, here), (low, 1 - here), (1 - low, 1 - here))
        for ref, (l, side) in zip((own_ref, p1, p2, p3), spots):
            ref[:, g * SLIM : (g + 1) * SLIM] = hold_ref[g, l, side].astype(ref.dtype)


def last_kernel(factor, kept_ref, r1, r2, r3, one_ref, two_ref):
    total = kept_ref[...]
    for ref in (r1, r2, r3):
        total = total + ref[...].astype(F32)
    total = total * factor
    total = total.T
    one_ref[...] = total[0:SLIM]
    two_ref[...] = total[SLIM : 2 * SLIM]


def parcels_of(dims):
    return [shape_of(dims, F32), shape_of(dims, F32), shape_of((2, *dims), BF16)]


def pieces_of(dims):
    return [shape_of(dims, F32)] + [shape_of(dims, BF16)] * 3


def swap_core(block):
    return send(block, lambda x, y, l, h, c: (x, y, l, h, 1 - c))


def along(axis, step):
    def move(x, y, l, h, c):
        flip = (1 + 2 * c, 3 - 2 * c)[step]
        z = l + 2 * h
        if axis == "x":
            x = x ^ flip
        elif axis == "y":
            y = y ^ flip
        else:
            z = z ^ flip
        return x, y, z % 2, z // 2, c

    return move


def exchange(pieces, axis):
    own, other, parcel = pieces
    got = send(parcel, along(axis, 0))
    parcel = call(middle_kernel, shape_of(own.shape, BF16), (other, got))
    return own, got, send(parcel, along(axis, 1))


def second_stage(turned, held):
    dims = (TALL, 8 * SLIM)
    return call(
        functools.partial(second_kernel, turned),
        pieces_of(dims),
        held,
        scratch=[pltpu.VMEM((4, *dims), F32)],
    )


def over(pieces, axis):
    own, *pieces = pieces
    result = [own]
    for k, piece in enumerate(pieces):
        if axis == "x":
            result.append(send(piece, lambda x, y, l, h, c: (x + k + 1, y, l, h, c)))
        else:
            result.append(send(piece, lambda x, y, l, h, c: (x, y + k + 1, l, h, c)))
    return result


def reduce_grads(full_one, send_one, full_two, send_two, factor):
    got_one = swap_core(send_one)
    got_two = swap_core(send_two)
    dims = (2, BLOCK, CH)
    one = call(
        one_first_kernel,
        parcels_of(dims),
        (full_one, got_one),
        scratch=[pltpu.VMEM((4, *dims), F32)],
    )
    two = call(two_first_kernel, parcels_of(dims), (full_two, got_two))
    one = second_stage(True, exchange(one, "x"))
    two = second_stage(False, exchange(two, "y"))
    one = over(one, "y")
    two = over(two, "x")
    dims = (BLOCK, 2 * SLIM)
    own, *pieces = call(
        third_kernel,
        pieces_of(dims),
        (*one, *two),
        scratch=[pltpu.VMEM((2, 2, 2, BLOCK, SLIM), F32)],
    )
    moves = (
        lambda x, y, l, h, c: (x, y, 1 - l, h, c),
        lambda x, y, l, h, c: (x, y, l, 1 - h, c),
        lambda x, y, l, h, c: (x, y, 1 - l, 1 - h, c),
    )
    got = []
    for piece, move in zip(pieces, moves):
        got.append(send(piece, move))
    kind = shape_of((SLIM, BLOCK), F32)
    one, two = call(functools.partial(last_kernel, factor), [kind, kind], (own, *got))
    return one.T, two.T


def swap_chip(block):
    return send(block, lambda x, y, l, h, c: (x, y, l, h, 1 - c))


def swap_distant(block):
    count = lax.axis_size("rows")
    pairs = [(i, i + 1) for i in range(1, count - 1, 2)]
    return lax.ppermute(block, "rows", pairs + [(j, i) for i, j in pairs])


def swap_in_steps(block):
    count = lax.axis_size("rows")
    pairs = [(i, i) for i in range(count) if i % 4 in (1, 2)]
    for i in range(3, count - 1, 4):
        pairs += [(i, i + 4), (i + 1, i - 3)]
    block = lax.ppermute(block, "rows", pairs)
    return lax.ppermute(block, "rows", [(i, i ^ 3) for i in range(count)])


def on_device(inputs, cotangent, weight_one, weight_two):
    picture = inputs[0]
    upstream = cotangent[0]
    factor = 1.0 / math.sqrt(lax.axis_size("dp") * ROWS * lax.axis_size("rows") * COLS)
    work = 2 * ROWS * COLS * CH * CH
    first_core = lax.rem(lax.axis_index("rows"), 2) == 0
    head, tail = picture[:4], picture[-4:]
    edge_distant = swap_distant(jnp.where(first_core, head, tail))
    edge_chip = swap_chip(jnp.where(first_core, tail, head))
    part_kinds = [shape_of((count, COLS, CH), BF16) for _, count in PARTS]
    c_parts = [swap_distant(upstream[first : first + count]) for first, count in PARTS]
    c_chip = swap_chip(upstream)
    kind = shape_of((6 * CH, 2 * CH), BF16)
    forward_w, backward_w = call(weight_kernel, [kind, kind], (weight_two,))
    map_kind = shape_of((ROWS, COLS, CH), BF16)
    sum_kind = shape_of((ROWS, COLS, CH), F32)
    wide_kind = shape_of((3, ROWS + 8, COLS, CH), BF16)
    hidden, near, weight_one = call(
        near_mid_kernel,
        [map_kind, wide_kind, shape_of((TAPS, CH), BF16)],
        (picture, pltpu.with_memory_space_constraint(weight_one, pltpu.HBM)),
        flops=7 * work,
        scratch=[pltpu.SemaphoreType.DMA],
        where=[WHOLE, pl.BlockSpec(memory_space=pltpu.HBM)],
    )
    hidden, near = call(
        near_edge_kernel,
        [map_kind, wide_kind],
        (edge_distant, edge_chip, weight_one, hidden, near),
        flops=2 * work,
        aliases={3: 0, 4: 1},
    )
    h_chip = swap_chip(hidden)
    h_distant = swap_in_steps(hidden)
    halves = [pltpu.VMEM((ROWS * HALF, 2 * CH), BF16)] * 2
    full_kind = shape_of((TAPS, CH), F32)
    send_kind = shape_of((4, 2, BLOCK, CH), BF16)
    begun = call(
        grad_start_kernel,
        shape_of((TAPS, CH), F32),
        (hidden, upstream, c_chip),
        flops=4 * work,
        scratch=halves,
    )
    back = call(
        functools.partial(far_start_kernel, True),
        sum_kind,
        (upstream, c_chip, backward_w),
        flops=4 * work,
    )
    result = call(
        functools.partial(far_start_kernel, False),
        sum_kind,
        (hidden, h_chip, forward_w),
        flops=4 * work,
    )
    last = len(PARTS) - 1
    full_one, full_two = None, begun
    for i, (first, count) in enumerate(PARTS):
        share = count * work // ROWS
        masked = call(
            functools.partial(back_end_kernel, first, count),
            part_kinds[i],
            (back, c_parts[i], backward_w, hidden),
            flops=2 * share,
        )
        kinds = [full_kind, send_kind] if i == last else [full_kind]
        near_out = call(
            functools.partial(near_part_kernel, first, count),
            kinds,
            (near, masked) if i == 0 else (near, masked, full_one),
            flops=9 * share,
            aliases={} if i == 0 else {2: 0},
        )
        full_one = near_out[0]
        grad_out = call(
            functools.partial(grad_part_kernel, first),
            kinds,
            (hidden, c_parts[i], full_two),
            flops=2 * share,
            scratch=[pltpu.VMEM((count * HALF, 2 * CH), BF16)] * 2,
            aliases={2: 0},
        )
        full_two = grad_out[0]
    grad_one, grad_two = reduce_grads(full_one, near_out[1], full_two, grad_out[1], factor)
    output = call(conv_end_kernel, map_kind, (result, h_distant, forward_w), flops=2 * work)
    return (output[None], grad_one, grad_two)


def solution(mesh):
    return jax.shard_map(
        on_device,
        mesh=mesh,
        in_specs=(P("dp", "rows", None, None), P("dp", "rows", None, None), P(), P()),
        out_specs=(P("dp", "rows", None, None), P("rows", "dp"), P("rows", "dp")),
        check_vma=False,
    )
```

```python
import functools
import math

import jax
import jax.numpy as jnp
from jax import lax
from jax.experimental import pallas as pl
from jax.experimental.pallas import tpu as pltpu
from jax.sharding import PartitionSpec as P


F32 = jnp.float32
BF16 = jnp.bfloat16
CH = 384
ROWS = 32
COLS = 64
HALF = 32
TAPS = 9 * CH
BLOCK = 216
SLIM = 48
TALL = 112
WHOLE = pl.BlockSpec(memory_space=pltpu.VMEM)
PARTS = ((0, 16), (16, 8), (24, 8))
AXES = ("dp", "rows")


def call(kernel, outs, args, flops=0, scratch=(), limit=8, aliases=None, where=None):
    single = not isinstance(outs, (list, tuple))
    shapes = [outs] if single else list(outs)
    moved = sum(a.size * a.dtype.itemsize for a in list(args) + shapes)
    run = pl.pallas_call(
        kernel,
        out_shape=shapes,
        in_specs=where or [WHOLE] * len(args),
        out_specs=[WHOLE] * len(shapes),
        scratch_shapes=list(scratch),
        input_output_aliases=aliases or {},
        compiler_params=pltpu.CompilerParams(vmem_limit_bytes=limit << 20),
        cost_estimate=pl.CostEstimate(flops=flops, bytes_accessed=moved, transcendentals=0),
    )
    result = run(*args)
    return result[0] if single else result


def shape_of(dims, kind):
    return jax.ShapeDtypeStruct(dims, kind)


def matmul(left, right):
    return jnp.dot(left, right, preferred_element_type=F32)


def place():
    dp = lax.axis_index("dp")
    rows = lax.axis_index("rows")
    return (
        lax.rem(dp, 4),
        lax.div(rows, 4),
        lax.rem(lax.div(rows, 2), 2),
        lax.div(dp, 4),
        lax.rem(rows, 2),
    )


def pairs_of(move):
    found = []
    for x in range(4):
        for y in range(4):
            for low in range(2):
                for high in range(2):
                    for core in range(2):
                        tx, ty, tl, th, tc = move(x, y, low, high, core)
                        source = (high * 4 + x) * 16 + (y * 2 + low) * 2 + core
                        target = (th * 4 + tx % 4) * 16 + ((ty % 4) * 2 + tl) * 2 + tc
                        found.append((source, target))
    return found


def send(block, move):
    return lax.ppermute(block, AXES, pairs_of(move))


def stage_kernel(picture_ref, upstream_ref, distant_ref, chip_ref, part_ref, sems):
    core = place()[4]
    edge = ROWS - 4
    copies = (
        pltpu.make_async_copy(picture_ref.at[pl.ds(edge * core, 4)], distant_ref, sems.at[0]),
        pltpu.make_async_copy(picture_ref.at[pl.ds(edge * (1 - core), 4)], chip_ref, sems.at[1]),
        pltpu.make_async_copy(upstream_ref.at[pl.ds(0, PARTS[0][1])], part_ref, sems.at[2]),
    )
    for copy in copies:
        copy.start()
    for copy in copies:
        copy.wait()


def weight_kernel(w_ref, forward_ref, backward_ref):
    for a in range(3):
        zero = w_ref[pl.ds((3 * a + 1) * CH, CH)]
        minus = w_ref[pl.ds(3 * a * CH, CH)]
        plus = w_ref[pl.ds((3 * a + 2) * CH, CH)]
        parts = ((zero, minus), (plus, zero))
        for i in range(2):
            for j in range(2):
                forward_ref[pl.ds((2 * a + i) * CH, CH), pl.ds(j * CH, CH)] = parts[i][j]
                backward_ref[pl.ds((2 * a + j) * CH, CH), pl.ds(i * CH, CH)] = parts[i][j].T


def shifted_store(near_ref, first, value):
    count = value.shape[0]
    zeros = jnp.zeros((count, 4, CH), BF16)
    near_ref[0, pl.ds(first, count)] = jnp.concatenate([zeros, value[:, : COLS - 4]], axis=1)
    near_ref[1, pl.ds(first, count)] = value
    near_ref[2, pl.ds(first, count)] = jnp.concatenate([value[:, 4:], zeros], axis=1)


def near_rows(near_ref, w_ref, hidden_ref, first, count):
    total = None
    for a in range(3):
        for b in range(3):
            window = near_ref[b, pl.ds(first + 4 * a, count)].reshape(count * COLS, CH)
            product = matmul(window, w_ref[pl.ds((3 * a + b) * CH, CH)])
            total = product if total is None else total + product
    hidden_ref[pl.ds(first, count)] = (
        jnp.maximum(total, 0.0).astype(BF16).reshape(count, COLS, CH)
    )


def near_mid_kernel(own_ref, far_ref, hidden_ref, near_ref, w_ref, sem):
    copy = pltpu.make_async_copy(far_ref, w_ref, sem)
    copy.start()

    @pl.loop(0, ROWS // 4)
    def _(i):
        shifted_store(near_ref, 4 + i * 4, own_ref[pl.ds(i * 4, 4)])

    copy.wait()

    @pl.loop(0, 3)
    def _(m):
        near_rows(near_ref, w_ref, hidden_ref, 4 + m * 8, 8)


def near_edge_kernel(distant_ref, chip_ref, w_ref, mid_ref, wide_ref, hidden_ref, near_ref):
    core = place()[4]
    shifted_store(near_ref, (ROWS + 4) * core, distant_ref[...])
    shifted_store(near_ref, (ROWS + 4) * (1 - core), chip_ref[...])

    @pl.loop(0, 2)
    def _(m):
        near_rows(near_ref, w_ref, hidden_ref, m * (ROWS - 4), 4)


def side_rows(ref, first, chunk):
    return jnp.concatenate(
        [
            ref[pl.ds(first, chunk), pl.ds(side * HALF, HALF)].reshape(chunk * HALF, CH)
            for side in range(2)
        ],
        axis=1,
    )


def block_of(w_ref, at):
    return w_ref[pl.ds(pl.multiple_of(at * 2 * CH, 16), 2 * CH)]


def far_start_kernel(flip, own_ref, chip_ref, w_ref, total_ref):
    core = place()[4]
    at = 2 * core if flip else 2 - 2 * core
    chunk = 16

    @pl.loop(0, ROWS // chunk)
    def _(m):
        total = matmul(side_rows(own_ref, m * chunk, chunk), block_of(w_ref, 1))
        total = total + matmul(side_rows(chip_ref, m * chunk, chunk), block_of(w_ref, at))
        for side in range(2):
            total_ref[pl.ds(m * chunk, chunk), pl.ds(side * HALF, HALF)] = total[
                :, side * CH : (side + 1) * CH
            ].reshape(chunk, HALF, CH)


def distant_part(distant_ref, w_ref, at, first, chunk):
    return matmul(side_rows(distant_ref, first, chunk), block_of(w_ref, at))


def conv_end_kernel(total_ref, distant_ref, w_ref, out_ref):
    core = place()[4]
    chunk = 16

    @pl.loop(0, ROWS // chunk)
    def _(m):
        total = distant_part(distant_ref, w_ref, 2 * core, m * chunk, chunk)
        for side in range(2):
            where = (pl.ds(m * chunk, chunk), pl.ds(side * HALF, HALF))
            part = total[:, side * CH : (side + 1) * CH].reshape(chunk, HALF, CH)
            out_ref[where] = (total_ref[where] + part).astype(BF16)


def back_end_kernel(first, count, total_ref, distant_ref, w_ref, hidden_ref, out_ref):
    core = place()[4]
    total = distant_part(distant_ref, w_ref, 2 - 2 * core, 0, count)
    for side in range(2):
        cols = slice(side * HALF, (side + 1) * HALF)
        where = (slice(first, first + count), cols)
        part = total[:, side * CH : (side + 1) * CH].reshape(count, HALF, CH)
        value = (total_ref[where] + part).astype(BF16)
        out_ref[:, cols] = jnp.where(hidden_ref[where] > 0, value, jnp.zeros_like(value))


def block_at(full_ref, y, low, core, at=0, count=BLOCK):
    first = pl.multiple_of((4 * y + 2 * low + core) * BLOCK + at, 8)
    return full_ref[pl.ds(first, count)]


def fill_send(full_ref, send_ref):
    core = place()[4]
    for y in range(4):
        for low in range(2):
            send_ref[y, low] = block_at(full_ref, y, low, 1 - core).astype(BF16)


def outer(left, right):
    return lax.dot_general(left, right, (((0,), (0,)), ((), ())), preferred_element_type=F32)


def fill_halves(ref, out_ref):
    for side in range(2):
        out_ref[:, side * CH : (side + 1) * CH] = ref[
            :, side * HALF : (side + 1) * HALF
        ].reshape(ROWS * HALF, CH)


def taps_at(full_ref, at):
    return full_ref.at[pl.ds(pl.multiple_of(at * 3 * CH, 16), 3 * CH)]


def outer_taps(h_ref, c_ref, target):
    grad = outer(h_ref[...], c_ref[...])
    target[0:CH] = grad[:CH, CH:]
    target[CH : 2 * CH] = grad[:CH, :CH] + grad[CH:, CH:]
    target[2 * CH :] = grad[CH:, :CH]


def grad_start_kernel(hidden_ref, own_ref, chip_ref, full_ref, h_ref, c_ref):
    core = place()[4]
    fill_halves(hidden_ref, h_ref)
    fill_halves(own_ref, c_ref)
    outer_taps(h_ref, c_ref, taps_at(full_ref, 1))
    fill_halves(chip_ref, c_ref)
    outer_taps(h_ref, c_ref, taps_at(full_ref, 2 * core))


def fill_part(ref, first, out_ref):
    count = out_ref.shape[0] // HALF
    for side in range(2):
        out_ref[:, side * CH : (side + 1) * CH] = ref[
            first : first + count, side * HALF : (side + 1) * HALF
        ].reshape(count * HALF, CH)


def grad_part_kernel(first, hidden_ref, distant_ref, begun_ref, full_ref, *refs):
    core = place()[4]
    h_ref, c_ref = refs[-2:]
    fill_part(hidden_ref, first, h_ref)
    fill_part(distant_ref, 0, c_ref)
    grad = outer(h_ref[...], c_ref[...])
    target = taps_at(full_ref, 2 - 2 * core)
    terms = (grad[:CH, CH:], grad[:CH, :CH] + grad[CH:, CH:], grad[CH:, :CH])
    for b, term in enumerate(terms):
        where = slice(b * CH, (b + 1) * CH)
        target[where] = target[where] + term if first else term
    if len(refs) == 3:
        fill_send(full_ref, refs[0])


def near_part_kernel(first, count, near_ref, masked_ref, *refs):
    if first:
        refs = refs[1:]
    full_ref = refs[0]
    target = masked_ref[...].reshape(count * COLS, CH)
    for a in range(3):
        for b in range(3):
            start = 4 * a + first
            window = near_ref[b, start : start + count].reshape(count * COLS, CH)
            where = pl.ds((3 * a + b) * CH, CH)
            term = outer(window, target)
            full_ref[where] = full_ref[where] + term if first else term
    if len(refs) == 2:
        fill_send(full_ref, refs[1])


BANDS = tuple((at, min(48, BLOCK - at)) for at in range(0, BLOCK, 48))


def partners(spot, core):
    return spot ^ (1 + 2 * core), spot ^ (3 - 2 * core), spot ^ 2


def hand_out(piece, spot, core, own_ref, other_ref, send_ref):
    near, later, across = partners(spot, core)
    own_ref[...] = piece(spot)
    other_ref[...] = piece(later)
    send_ref[0] = piece(near).astype(BF16)
    send_ref[1] = piece(across).astype(BF16)


def one_first_kernel(full_ref, got_ref, own_ref, other_ref, send_ref, hold_ref):
    x, _, _, _, core = place()
    for at, count in BANDS:
        band = slice(at, at + count)
        lane = lax.broadcasted_iota(jnp.int32, (count, CH), 1)
        lane = jnp.where(lane >= 4 * SLIM, lane - 4 * SLIM, lane)
        for low in range(2):
            turned = []
            for y in range(4):
                total = block_at(full_ref, y, low, core, at, count)
                total = total + got_ref[y, low, band].astype(F32)
                turned.append(pltpu.roll(total, SLIM * y, 1) if y else total)
            for q in range(4):
                part = turned[(3 - q) % 4]
                for r in (2, 1, 0):
                    part = jnp.where(lane < (r + 1) * SLIM, turned[(r - q) % 4], part)
                hold_ref[q, low, band] = part
    hand_out(lambda q: hold_ref[q], x, core, own_ref, other_ref, send_ref)


def two_first_kernel(full_ref, got_ref, own_ref, other_ref, send_ref):
    _, y, _, _, core = place()
    near, later, across = partners(y, core)
    spots = ((own_ref, y), (other_ref, later), (send_ref.at[0], near), (send_ref.at[1], across))
    for ref, at in spots:
        for low in range(2):
            total = block_at(full_ref, at, low, core) + got_ref[at, low].astype(F32)
            ref[low] = total.astype(ref.dtype)


def middle_kernel(other_ref, got_ref, out_ref):
    out_ref[...] = (other_ref[...] + got_ref[1].astype(F32)).astype(BF16)


PACKS = ((0, 48), (48, 48), (96, 16), (112, 48), (160, 48), (208, 8))


def second_kernel(turned, kept_ref, got_ref, last_ref, own_ref, p1, p2, p3, hold_ref):
    x, y = place()[:2]
    base = x + y if turned else x
    for at, count in PACKS:
        band = slice(at, at + count)
        right = at >= TALL
        rows = slice(at - TALL, at - TALL + count) if right else band
        for low in range(2):
            total = kept_ref[low, band] + got_ref[0, low, band].astype(F32)
            total = total + last_ref[low, band].astype(F32)
            for q in range(4):
                for side in range(2):
                    start = side * 4 * SLIM + q * SLIM
                    to = (4 * right + 2 * low + side) * SLIM
                    hold_ref[q, rows, to : to + SLIM] = total[:, start : start + SLIM]
    own_ref[...] = hold_ref[lax.rem(base, 4)]
    for k, ref in enumerate((p1, p2, p3)):
        ref[...] = hold_ref[lax.rem(base + k + 1, 4)].astype(BF16)


def third_kernel(*refs):
    ins, (own_ref, p1, p2, p3, hold_ref) = refs[:8], refs[8:]
    x, y, low, high, _ = place()
    for g in range(2):
        kept, *got = ins[4 * g : 4 * g + 4]
        total = kept[...]
        for ref in got:
            total = total + ref[...].astype(F32)
        for l in range(2):
            for side in range(2):
                at = (2 * l + side) * SLIM
                hold_ref[g, l, side, 0:TALL] = total[:, at : at + SLIM]
                at = at + 4 * SLIM
                hold_ref[g, l, side, TALL:BLOCK] = total[: BLOCK - TALL, at : at + SLIM]
        here = high if g else lax.rem(high + lax.div(x + y, 4), 2)
        spots = ((low, here), (1 - low, here), (low, 1 - here), (1 - low, 1 - here))
        for ref, (l, side) in zip((own_ref, p1, p2, p3), spots):
            ref[:, g * SLIM : (g + 1) * SLIM] = hold_ref[g, l, side].astype(ref.dtype)


def last_kernel(factor, kept_ref, r1, r2, r3, one_ref, two_ref):
    total = kept_ref[...]
    for ref in (r1, r2, r3):
        total = total + ref[...].astype(F32)
    total = total * factor
    total = total.T
    one_ref[...] = total[0:SLIM]
    two_ref[...] = total[SLIM : 2 * SLIM]


def parcels_of(dims):
    return [shape_of(dims, F32), shape_of(dims, F32), shape_of((2, *dims), BF16)]


def pieces_of(dims):
    return [shape_of(dims, F32)] + [shape_of(dims, BF16)] * 3


def swap_core(block):
    return send(block, lambda x, y, l, h, c: (x, y, l, h, 1 - c))


def along(axis, step):
    def move(x, y, l, h, c):
        flip = (1 + 2 * c, 3 - 2 * c)[step]
        z = l + 2 * h
        if axis == "x":
            x = x ^ flip
        elif axis == "y":
            y = y ^ flip
        else:
            z = z ^ flip
        return x, y, z % 2, z // 2, c

    return move


def exchange(pieces, axis):
    own, other, parcel = pieces
    got = send(parcel, along(axis, 0))
    parcel = call(middle_kernel, shape_of(own.shape, BF16), (other, got))
    return own, got, send(parcel, along(axis, 1))


def second_stage(turned, held):
    dims = (TALL, 8 * SLIM)
    return call(
        functools.partial(second_kernel, turned),
        pieces_of(dims),
        held,
        scratch=[pltpu.VMEM((4, *dims), F32)],
    )


def over(pieces, axis):
    own, *pieces = pieces
    result = [own]
    for k, piece in enumerate(pieces):
        if axis == "x":
            result.append(send(piece, lambda x, y, l, h, c: (x + k + 1, y, l, h, c)))
        else:
            result.append(send(piece, lambda x, y, l, h, c: (x, y + k + 1, l, h, c)))
    return result


def reduce_grads(full_one, send_one, full_two, send_two, factor):
    got_one = swap_core(send_one)
    got_two = swap_core(send_two)
    dims = (2, BLOCK, CH)
    one = call(
        one_first_kernel,
        parcels_of(dims),
        (full_one, got_one),
        scratch=[pltpu.VMEM((4, *dims), F32)],
    )
    two = call(two_first_kernel, parcels_of(dims), (full_two, got_two))
    one = second_stage(True, exchange(one, "x"))
    two = second_stage(False, exchange(two, "y"))
    one = over(one, "y")
    two = over(two, "x")
    dims = (BLOCK, 2 * SLIM)
    own, *pieces = call(
        third_kernel,
        pieces_of(dims),
        (*one, *two),
        scratch=[pltpu.VMEM((2, 2, 2, BLOCK, SLIM), F32)],
    )
    moves = (
        lambda x, y, l, h, c: (x, y, 1 - l, h, c),
        lambda x, y, l, h, c: (x, y, l, 1 - h, c),
        lambda x, y, l, h, c: (x, y, 1 - l, 1 - h, c),
    )
    got = []
    for piece, move in zip(pieces, moves):
        got.append(send(piece, move))
    kind = shape_of((SLIM, BLOCK), F32)
    one, two = call(functools.partial(last_kernel, factor), [kind, kind], (own, *got))
    return one.T, two.T


def swap_chip(block):
    return send(block, lambda x, y, l, h, c: (x, y, l, h, 1 - c))


def swap_distant(block):
    count = lax.axis_size("rows")
    pairs = [(i, i + 1) for i in range(1, count - 1, 2)]
    return lax.ppermute(block, "rows", pairs + [(j, i) for i, j in pairs])


def swap_in_steps(block):
    count = lax.axis_size("rows")
    pairs = [(i, i) for i in range(count) if i % 4 in (1, 2)]
    for i in range(3, count - 1, 4):
        pairs += [(i, i + 4), (i + 1, i - 3)]
    block = lax.ppermute(block, "rows", pairs)
    return lax.ppermute(block, "rows", [(i, i ^ 3) for i in range(count)])


def on_device(inputs, cotangent, weight_one, weight_two):
    picture = inputs[0]
    upstream = cotangent[0]
    factor = 1.0 / math.sqrt(lax.axis_size("dp") * ROWS * lax.axis_size("rows") * COLS)
    work = 2 * ROWS * COLS * CH * CH
    part_kinds = [shape_of((count, COLS, CH), BF16) for _, count in PARTS]
    edge_kind = shape_of((4, COLS, CH), BF16)
    edge_distant, edge_chip, first_part = call(
        stage_kernel,
        [edge_kind, edge_kind, part_kinds[0]],
        [pltpu.with_memory_space_constraint(a, pltpu.HBM) for a in (picture, upstream)],
        scratch=[pltpu.SemaphoreType.DMA((3,))],
        where=[pl.BlockSpec(memory_space=pltpu.HBM)] * 2,
    )
    edge_distant = swap_distant(edge_distant)
    edge_chip = swap_chip(edge_chip)
    c_parts = [first_part] + [upstream[first : first + count] for first, count in PARTS[1:]]
    c_parts = [swap_distant(part) for part in c_parts]
    c_chip = swap_chip(upstream)
    kind = shape_of((6 * CH, 2 * CH), BF16)
    forward_w, backward_w = call(weight_kernel, [kind, kind], (weight_two,))
    map_kind = shape_of((ROWS, COLS, CH), BF16)
    sum_kind = shape_of((ROWS, COLS, CH), F32)
    wide_kind = shape_of((3, ROWS + 8, COLS, CH), BF16)
    hidden, near, weight_one = call(
        near_mid_kernel,
        [map_kind, wide_kind, shape_of((TAPS, CH), BF16)],
        (picture, pltpu.with_memory_space_constraint(weight_one, pltpu.HBM)),
        flops=7 * work,
        scratch=[pltpu.SemaphoreType.DMA],
        where=[WHOLE, pl.BlockSpec(memory_space=pltpu.HBM)],
    )
    hidden, near = call(
        near_edge_kernel,
        [map_kind, wide_kind],
        (edge_distant, edge_chip, weight_one, hidden, near),
        flops=2 * work,
        aliases={3: 0, 4: 1},
    )
    h_chip = swap_chip(hidden)
    h_distant = swap_in_steps(hidden)
    halves = [pltpu.VMEM((ROWS * HALF, 2 * CH), BF16)] * 2
    full_kind = shape_of((TAPS, CH), F32)
    send_kind = shape_of((4, 2, BLOCK, CH), BF16)
    begun = call(
        grad_start_kernel,
        shape_of((TAPS, CH), F32),
        (hidden, upstream, c_chip),
        flops=4 * work,
        scratch=halves,
    )
    back = call(
        functools.partial(far_start_kernel, True),
        sum_kind,
        (upstream, c_chip, backward_w),
        flops=4 * work,
    )
    result = call(
        functools.partial(far_start_kernel, False),
        sum_kind,
        (hidden, h_chip, forward_w),
        flops=4 * work,
    )
    last = len(PARTS) - 1
    full_one, full_two = None, begun
    for i, (first, count) in enumerate(PARTS):
        share = count * work // ROWS
        masked = call(
            functools.partial(back_end_kernel, first, count),
            part_kinds[i],
            (back, c_parts[i], backward_w, hidden),
            flops=2 * share,
        )
        kinds = [full_kind, send_kind] if i == last else [full_kind]
        near_out = call(
            functools.partial(near_part_kernel, first, count),
            kinds,
            (near, masked) if i == 0 else (near, masked, full_one),
            flops=9 * share,
            aliases={} if i == 0 else {2: 0},
        )
        full_one = near_out[0]
        grad_out = call(
            functools.partial(grad_part_kernel, first),
            kinds,
            (hidden, c_parts[i], full_two),
            flops=2 * share,
            scratch=[pltpu.VMEM((count * HALF, 2 * CH), BF16)] * 2,
            aliases={2: 0},
        )
        full_two = grad_out[0]
    grad_one, grad_two = reduce_grads(full_one, near_out[1], full_two, grad_out[1], factor)
    output = call(conv_end_kernel, map_kind, (result, h_distant, forward_w), flops=2 * work)
    return (output[None], grad_one, grad_two)


def solution(mesh):
    return jax.shard_map(
        on_device,
        mesh=mesh,
        in_specs=(P("dp", "rows", None, None), P("dp", "rows", None, None), P(), P()),
        out_specs=(P("dp", "rows", None, None), P("rows", "dp"), P("rows", "dp")),
        check_vma=False,
    )
```
